1024 devices in a mesh: ctx: 64 (over x, z), fsdp: 16 (over y, core).
Axes of the slice: x: 4, y: 8, z: 16, core: 2. Of those that a mesh axis runs over, the one named last changes fastest.
Arguments:
- inputs: bfloat16 [8192, 8192], P('ctx', 'fsdp'), may hold values from -6 to 6
- upstream: bfloat16 [8192, 8192], P('ctx', 'fsdp'), may hold values from -6 to 6
- medium_filter: bfloat16 [512, 128], P('fsdp'), may hold values from -0.5 to 0.5
- short_filter: bfloat16 [512, 7], P('fsdp'), may hold values from -2 to 2
Outputs:
- input_gradient: bfloat16 [8192, 8192], P('ctx', 'fsdp')
- medium_gradient: float32 [512, 128], P('fsdp')
- short_gradient: float32 [512, 7], P('fsdp')
The draws below stay inside these ranges and needn't reach their ends.
All inputs are finite; a program needn't handle non-finite values.
Results may differ from the reference program's by a relative error of at most 0.005.
Values may be sent and summed in bfloat16 or wider, within the bound.
A program may use at most 64 MiB of HBM per device.

```python
import math
import jax
import jax.numpy as jnp
from jax import lax

C = 8192
GROUP = 16
MED = 128
SHORT = 7
GROUPS = 512
LEN = 8192


def block_scale(rng, extent, shards, least, top_value):
    def one(dim, shards_of):
        draws = jax.random.uniform(jax.random.fold_in(jax.random.fold_in(rng, 6), dim), (shards_of,), jnp.float32, least / len(shards), top_value / len(shards))
        return jnp.repeat(jnp.exp(draws), extent[dim] // shards_of).reshape((-1,) + (1,) * (len(extent) - dim - 1))

    factor_of = one(*shards[0])
    for cut in shards[1:]:
        factor_of = factor_of * one(*cut)
    return factor_of


def centred(key, extent, scale, most, cuts=(), dtype=jnp.bfloat16):
    level = block_scale(key, extent, cuts, -0.22, 0.18) if cuts else 1.0
    drawn = jax.random.normal(key, extent, jnp.float32) * scale * level
    return jnp.minimum(jnp.maximum(drawn, -most), most).astype(dtype)


def setup_inputs(seed: int = 0) -> dict:
    seeds = jax.random.split(jax.random.key(seed), 5)
    return {
        "inputs": centred(seeds[0], (LEN, C), 1.0, 6.0, ((0, 64), (1, 16))),
        "upstream": centred(seeds[1], (LEN, C), 1.0, 6.0, ((0, 64), (1, 16))),
        "medium_filter": centred(seeds[2], (GROUPS, MED), MED ** -0.5, 0.5, ((0, 16),)),
        "short_filter": centred(seeds[3], (GROUPS, SHORT), SHORT ** -0.5, 2.0, ((0, 16),)),
    }


def reference(inputs, upstream, medium_filter, short_filter):
    block_width = math.gcd(C, 256)
    block_groups = block_width // GROUP
    block_count = C // block_width
    fft_points = 2 * LEN

    def one_block(index, carry):
        grads, medium_total, short_total = carry
        start = (index * block_width).astype(jnp.int32)
        row_start = (index * block_groups).astype(jnp.int32)
        values = lax.dynamic_slice_in_dim(inputs, start, block_width, 1).astype(jnp.float32)
        cot_values = lax.dynamic_slice_in_dim(upstream, start, block_width, 1).astype(jnp.float32)
        medium_rows = lax.dynamic_slice_in_dim(medium_filter, row_start, block_groups, 0).astype(jnp.float32)
        short_rows_in = lax.dynamic_slice_in_dim(short_filter, row_start, block_groups, 0).astype(jnp.float32)
        medium_channel = jnp.repeat(medium_rows, GROUP, axis=0)
        short_channel = jnp.repeat(short_rows_in, GROUP, axis=0)
        medium_freq = jnp.fft.rfft(medium_channel.T, n=fft_points, axis=0)
        token_freq = jnp.fft.rfft(values, n=fft_points, axis=0)
        conv = jnp.fft.irfft(token_freq * medium_freq, n=fft_points, axis=0)[:LEN]
        gate = jnp.zeros((LEN, block_width), jnp.float32)
        for tap_index in range(SHORT):
            shifted = jnp.pad(values, ((tap_index, 0), (0, 0)))[:LEN]
            gate = gate + short_channel[:, tap_index] * shifted
        gate_cot = (cot_values * conv).astype(jnp.bfloat16)
        conv_cot = (cot_values * gate).astype(jnp.bfloat16)
        gate_vals = gate_cot.astype(jnp.float32)
        conv_vals = conv_cot.astype(jnp.float32)
        cot_freq = jnp.fft.rfft(conv_vals, n=fft_points, axis=0)
        medium_back = jnp.fft.irfft(cot_freq * jnp.conj(medium_freq), n=fft_points, axis=0)[:LEN]
        short_back = jnp.zeros((LEN, block_width), jnp.float32)
        short_terms = []
        for tap_index in range(SHORT):
            ahead = jnp.pad(gate_vals, ((0, tap_index), (0, 0)))[tap_index:]
            short_back = short_back + short_channel[:, tap_index] * ahead
            shifted = jnp.pad(values, ((tap_index, 0), (0, 0)))[:LEN]
            short_terms.append(jnp.sum(gate_vals * shifted, axis=0))
        gradient = (medium_back + short_back).astype(jnp.bfloat16)
        cross = jnp.fft.irfft(cot_freq * jnp.conj(token_freq), n=fft_points, axis=0)[:MED]
        medium_sum = jnp.sum(cross.reshape(MED, block_groups, GROUP), axis=2).T
        short_sum = jnp.sum(jnp.stack(short_terms, axis=0).reshape(SHORT, block_groups, GROUP), axis=2).T
        grads = lax.dynamic_update_slice_in_dim(grads, gradient, start, 1)
        medium_total = lax.dynamic_update_slice_in_dim(medium_total, medium_sum, row_start, 0)
        short_total = lax.dynamic_update_slice_in_dim(short_total, short_sum, row_start, 0)
        return grads, medium_total, short_total

    initial = (jnp.zeros((LEN, C), jnp.bfloat16), jnp.zeros((GROUPS, MED), jnp.float32), jnp.zeros((GROUPS, SHORT), jnp.float32))
    grads, medium_total, short_total = lax.fori_loop(0, block_count, one_block, initial)
    factor = float(GROUP * LEN) ** -0.5
    return grads, medium_total * factor, short_total * factor
```

```python
import functools

import jax
import jax.numpy as jnp
from jax import lax
from jax.experimental import pallas as pl
from jax.experimental.pallas import tpu as pltpu
from jax.sharding import PartitionSpec as P

GROUP = 16
ROWS = 128
LANES = 128
PER = LANES // GROUP
MESH = pl.DeviceIdType.MESH
NEAR = (1, -1, 2, -2, 3)
F32 = jnp.float32
BF16 = jnp.bfloat16


def nt(a, b):
    return lax.dot_general(a, b, (((1,), (1,)), ((), ())), preferred_element_type=F32)


def kernel(
    nx, nz, x_hbm, up_hbm, med_ref, short_ref, ig_hbm, tot_ref,
    xe, upv, cce, gce, igv, tf, tb, mrev, mfwd, sch, xf, sacc,
    rx, xs, rz, s5, s6, r2,
    load_sem, halo_send, halo_recv, back_send, back_recv,
    x_send, x_recv, z_send, z_recv, w_send, w_recv, out_sem, ready_a, ready_b,
):
    n = nx * nz
    width = xe.shape[1]
    blocks = width // LANES
    groups = width // GROUP
    taps = short_ref.shape[0]
    me = lax.axis_index("ctx")
    ix, iz = me // nz, lax.rem(me, nz)
    nxt, prv = lax.rem(me + 1, n), lax.rem(me + n - 1, n)

    def at_z(d):
        return {"ctx": ix * nz + lax.rem(iz + d + nz, nz)}

    def at_x(d):
        return {"ctx": lax.rem(ix + d + nx, nx) * nz + iz}

    def lanes(b):
        return pl.ds(pl.multiple_of(b * LANES, LANES), LANES)

    load_x = pltpu.make_async_copy(x_hbm, xe.at[pl.ds(ROWS, ROWS)], load_sem.at[0])
    load_u = pltpu.make_async_copy(up_hbm, upv, load_sem.at[1])
    load_x.start()
    load_u.start()

    barrier = pltpu.get_barrier_semaphore()
    near = [{"ctx": nxt}, {"ctx": prv}]
    near += [at_x(d) for d in range(1, nx)]
    near += [at_z(d) for d in (1, -1, 2, -2)]
    for peer in near:
        pl.semaphore_signal(barrier, inc=1, device_id=peer, device_id_type=MESH)
    pl.semaphore_wait(barrier, len(near))

    def halo(b):
        return pltpu.make_async_remote_copy(
            src_ref=x_hbm.at[:, lanes(b)],
            dst_ref=xe.at[pl.ds(0, ROWS), lanes(b)],
            send_sem=halo_send.at[b],
            recv_sem=halo_recv.at[b],
            device_id={"ctx": nxt},
            device_id_type=MESH,
        )

    @pl.when(me < n - 1)
    def _():
        for b in range(blocks):
            halo(b).start()

    for d in (2, -2):
        pl.semaphore_signal(ready_a, inc=1, device_id=at_z(d), device_id_type=MESH)

    rows2 = lax.broadcasted_iota(jnp.int32, (ROWS, LANES), 0)
    cols2 = lax.broadcasted_iota(jnp.int32, (ROWS, LANES), 1)
    lane_group = cols2 // GROUP

    flip = (rows2 + cols2 == LANES - 1).astype(BF16)
    mrev[...] = jnp.dot(med_ref[...], flip, preferred_element_type=F32)
    mfwd[...] = med_ref[...].astype(F32)
    chan = lax.broadcasted_iota(jnp.int32, (groups, width), 1) // GROUP
    own = lax.broadcasted_iota(jnp.int32, (groups, width), 0)
    spread = (chan == own).astype(BF16)
    sch[0:taps, :] = jnp.dot(short_ref[...], spread, preferred_element_type=F32)

    def forward_table(g, carry):
        row = jnp.broadcast_to(mrev[pl.ds(g, 1), :], (ROWS, LANES))
        turned = pltpu.roll(row, 1, 1, stride=1, stride_axis=0)
        top = pl.ds(pl.multiple_of(g * ROWS, ROWS), ROWS)
        tf[top, 0:LANES] = jnp.where(cols2 > rows2, turned, 0.0).astype(BF16)
        tf[top, LANES:] = jnp.where(cols2 <= rows2, turned, 0.0).astype(BF16)
        return carry

    lax.fori_loop(0, groups, forward_table, 0)

    pl.semaphore_wait(ready_a, 2)
    for d in (2, -2):
        pl.semaphore_signal(ready_b, inc=1, device_id=at_z(d), device_id_type=MESH)

    big_r = lax.broadcasted_iota(jnp.int32, (2 * ROWS, 2 * ROWS), 0)
    big_c = lax.broadcasted_iota(jnp.int32, (2 * ROWS, 2 * ROWS), 1)
    flip_rows = (big_r + big_c == 2 * ROWS - 1).astype(BF16)

    load_x.wait()
    load_u.wait()

    def block(b, carry):
        @pl.when(me > 0)
        def _():
            halo(b).wait_recv()

        @pl.when(me == 0)
        def _():
            xe[pl.ds(0, ROWS), lanes(b)] = jnp.zeros((ROWS, LANES), BF16)

        xb = xe[:, lanes(b)]
        xf[...] = xe[pl.ds(ROWS - 16, ROWS + 16), lanes(b)].astype(F32)
        gate = jnp.zeros((ROWS, LANES), F32)
        for j in range(taps):
            gate = gate + sch[j : j + 1, lanes(b)] * xf[16 - j : 16 - j + ROWS, :]
        conv = jnp.zeros((ROWS, LANES), F32)
        for k in range(PER):
            top = pl.ds(pl.multiple_of((b * PER + k) * ROWS, ROWS), ROWS)
            term = jnp.dot(tf[top, :], xb, preferred_element_type=F32)
            conv = jnp.where(lane_group == k, term, conv)
        up = upv[:, lanes(b)].astype(F32)
        gate_cot = (up * conv).astype(BF16)
        conv_cot = (up * gate).astype(BF16)
        cce[0:ROWS, lanes(b)] = conv_cot
        gce[0:ROWS, lanes(b)] = gate_cot
        gate_f = gate_cot.astype(F32)
        for j in range(taps):
            sacc[j : j + 1, lanes(b)] = jnp.sum(
                gate_f * xf[16 - j : 16 - j + ROWS, :], axis=0, keepdims=True
            )
        x_rev = jnp.dot(flip_rows, xb, preferred_element_type=F32).astype(BF16)
        for k in range(PER):
            part = jnp.where(lane_group == k, conv_cot, jnp.zeros((), BF16))
            pair = nt(part, x_rev)
            both = jnp.where(rows2 + cols2 >= LANES - 1, pair[:, :LANES], pair[:, LANES:])
            turned = pltpu.roll(both, 1, 1, stride=1, stride_axis=0)
            rx[ix, pl.ds(b * PER + k, 1), :] = jnp.sum(turned, axis=0, keepdims=True)
        return carry

    sacc[...] = jnp.zeros_like(sacc)
    lax.fori_loop(0, blocks, block, 0)

    tall_r = lax.broadcasted_iota(jnp.int32, (width, LANES), 0) // GROUP
    tall_c = lax.broadcasted_iota(jnp.int32, (width, LANES), 1)
    rx[ix, groups : groups + 8, :] = jnp.dot(
        sacc[...],
        (tall_r == tall_c).astype(F32),
        preferred_element_type=F32,
        precision=lax.Precision.HIGHEST,
    )

    def remote(src, dst, send, recv, peer):
        return pltpu.make_async_remote_copy(
            src_ref=src, dst_ref=dst, send_sem=send, recv_sem=recv, device_id=peer, device_id_type=MESH
        )

    pl.semaphore_wait(ready_b, 2)
    x_sends = [
        remote(rx.at[ix], rx.at[ix], x_send.at[d - 1], x_recv.at[d - 1], at_x(d)) for d in range(1, nx)
    ]
    for copy in x_sends:
        copy.start()

    back_c = remote(
        cce.at[pl.ds(0, ROWS)], cce.at[pl.ds(ROWS, ROWS)], back_send.at[0], back_recv.at[0], {"ctx": prv}
    )
    back_g = remote(
        gce.at[pl.ds(0, 16)], gce.at[pl.ds(ROWS, 16)], back_send.at[1], back_recv.at[1], {"ctx": prv}
    )

    @pl.when(me > 0)
    def _():
        back_g.start()
        back_c.start()

    def backward_table(g, carry):
        row = jnp.broadcast_to(mfwd[pl.ds(g, 1), :], (ROWS, LANES))
        turned = pltpu.roll(row, 0, 1, stride=1, stride_axis=0)
        top = pl.ds(pl.multiple_of(g * ROWS, ROWS), ROWS)
        tb[top, 0:LANES] = jnp.where(cols2 >= rows2, turned, 0.0).astype(BF16)
        tb[top, LANES:] = jnp.where(cols2 < rows2, turned, 0.0).astype(BF16)
        return carry

    lax.fori_loop(0, groups, backward_table, 0)

    for d in range(1, nx):
        source = lax.rem(ix - d + nx, nx)
        remote(rx.at[ix], rx.at[source], x_send.at[d - 1], x_recv.at[d - 1], at_x(d)).wait_recv()
    total = rx[0]
    for k in range(1, nx):
        total = total + rx[k]
    xs[...] = total
    z_sends = [remote(xs, rz.at[k], z_send.at[k], z_recv.at[k], at_z(-d)) for k, d in enumerate(NEAR)]
    for copy in z_sends:
        copy.start()
    for copy in z_sends[:4]:
        copy.wait_recv()
    five = ((rz[3] + rz[1]) + xs[...]) + (rz[0] + rz[2])
    s5[...] = five
    far_five = remote(s5, r2.at[0], w_send.at[0], w_recv.at[0], at_z(5))
    far_five.start()
    z_sends[4].wait_recv()
    s6[...] = five + rz[4]
    far_six = remote(s6, r2.at[1], w_send.at[1], w_recv.at[1], at_z(-5))
    far_six.start()

    @pl.when(me < n - 1)
    def _():
        back_g.wait_recv()
        back_c.wait_recv()

    @pl.when(me == n - 1)
    def _():
        cce[pl.ds(ROWS, ROWS), :] = jnp.zeros((ROWS, width), BF16)
        gce[pl.ds(ROWS, 16), :] = jnp.zeros((16, width), BF16)

    def store(b):
        return pltpu.make_async_copy(igv.at[:, lanes(b)], ig_hbm.at[:, lanes(b)], out_sem.at[b])

    def gradient(b, carry):
        cb = cce[:, lanes(b)]
        back = jnp.zeros((ROWS, LANES), F32)
        for k in range(PER):
            top = pl.ds(pl.multiple_of((b * PER + k) * ROWS, ROWS), ROWS)
            term = jnp.dot(tb[top, :], cb, preferred_element_type=F32)
            back = jnp.where(lane_group == k, term, back)
        xf[...] = gce[:, lanes(b)].astype(F32)
        short = jnp.zeros((ROWS, LANES), F32)
        for j in range(taps):
            short = short + sch[j : j + 1, lanes(b)] * xf[j : j + ROWS, :]
        igv[:, lanes(b)] = (back + short).astype(BF16)
        store(b).start()
        return carry

    lax.fori_loop(0, blocks, gradient, 0)

    far_five.wait_recv()
    far_six.wait_recv()
    tot_ref[...] = s5[...] + r2[0] + r2[1]

    for b in range(blocks):
        store(b).wait()

    @pl.when(me < n - 1)
    def _():
        for b in range(blocks):
            halo(b).wait_send()

    @pl.when(me > 0)
    def _():
        back_g.wait_send()
        back_c.wait_send()

    for copy in x_sends + z_sends + [far_five, far_six]:
        copy.wait_send()


def local(nx, nz, inputs, upstream, medium_filter, short_filter):
    rows, width = inputs.shape
    groups, taps = medium_filter.shape
    short_taps = short_filter.shape[1]
    if rows != ROWS or taps != LANES or width % LANES or groups != 32:
        raise ValueError("unsupported sizes")
    height = groups + 8
    blocks = width // LANES
    vmem = functools.partial(pltpu.VMEM)
    dma = pltpu.SemaphoreType.DMA
    gradient, total = pl.pallas_call(
        functools.partial(kernel, nx, nz),
        out_shape=(
            jax.ShapeDtypeStruct((rows, width), BF16),
            jax.ShapeDtypeStruct((height, LANES), F32),
        ),
        in_specs=[
            pl.BlockSpec(memory_space=pl.ANY),
            pl.BlockSpec(memory_space=pl.ANY),
            pl.BlockSpec(memory_space=pltpu.VMEM),
            pl.BlockSpec(memory_space=pltpu.VMEM),
        ],
        out_specs=(pl.BlockSpec(memory_space=pl.ANY), pl.BlockSpec(memory_space=pltpu.VMEM)),
        scratch_shapes=[
            vmem((2 * ROWS, width), BF16),
            vmem((ROWS, width), BF16),
            vmem((2 * ROWS, width), BF16),
            vmem((ROWS + 16, width), BF16),
            vmem((ROWS, width), BF16),
            vmem((groups * ROWS, 2 * LANES), BF16),
            vmem((groups * ROWS, 2 * LANES), BF16),
            vmem((groups, LANES), F32),
            vmem((groups, LANES), F32),
            vmem((8, width), F32),
            vmem((ROWS + 16, LANES), F32),
            vmem((8, width), F32),
            vmem((nx, height, LANES), F32),
            vmem((height, LANES), F32),
            vmem((len(NEAR), height, LANES), F32),
            vmem((height, LANES), F32),
            vmem((height, LANES), F32),
            vmem((2, height, LANES), F32),
            dma((2,)),
            dma((blocks,)),
            dma((blocks,)),
            dma((2,)),
            dma((2,)),
            dma((nx - 1,)),
            dma((nx - 1,)),
            dma((len(NEAR),)),
            dma((len(NEAR),)),
            dma((2,)),
            dma((2,)),
            dma((blocks,)),
            pltpu.SemaphoreType.REGULAR,
            pltpu.SemaphoreType.REGULAR,
        ],
        compiler_params=pltpu.CompilerParams(collective_id=0, has_side_effects=True),
    )(inputs, upstream, medium_filter, short_filter.T)
    factor = float(GROUP * rows * lax.axis_size("ctx")) ** (-0.5)
    medium = total[:groups] * factor
    short = total[groups : groups + short_taps, :groups].T * factor
    return gradient, medium, short


def solution(mesh):
    n = mesh.shape["ctx"]
    nz = 16
    return jax.shard_map(
        functools.partial(local, n // nz, nz),
        mesh=mesh,
        in_specs=(P("ctx", "fsdp"), P("ctx", "fsdp"), P("fsdp", None), P("fsdp", None)),
        out_specs=(P("ctx", "fsdp"), P("fsdp", None), P("fsdp", None)),
        check_vma=False,
    )
```

```python
import functools

import jax
import jax.numpy as jnp
from jax import lax
from jax.experimental import pallas as pl
from jax.experimental.pallas import tpu as pltpu
from jax.sharding import PartitionSpec as P

GROUP = 16
ROWS = 128
LANES = 128
PER = LANES // GROUP
MESH = pl.DeviceIdType.MESH
RAW = (1, 2, 3)
WIDE = (4, -4, 8)
F32 = jnp.float32
BF16 = jnp.bfloat16


def nt(a, b):
    return lax.dot_general(a, b, (((1,), (1,)), ((), ())), preferred_element_type=F32)


def kernel(
    nx, nz, x_hbm, up_hbm, med_hbm, short_hbm, igv, tot_ref,
    xe, upv, med_ref, short_ref, cce, gce, tf, tb, mrev, mfwd, sch, xf, sacc,
    rx, xs, rz, win, rw,
    load_sem, halo_send, halo_recv, back_send, back_recv,
    x_send, x_recv, z_send, z_recv, w_send, w_recv, go, across,
):
    n = nx * nz
    width = xe.shape[1]
    blocks = width // LANES
    groups = width // GROUP
    taps = short_ref.shape[0]
    me = lax.axis_index("ctx")
    ix, iz = me // nz, lax.rem(me, nz)

    def at_z(d):
        return ix, lax.rem(iz + d + nz, nz)

    def at_x(d):
        return lax.rem(ix + d + nx, nx), iz

    def at(d):
        other = lax.rem(me + d + n, n)
        return other // nz, lax.rem(other, nz)

    def ident(peer):
        return {"ctx": peer[0] * nz + peer[1]}

    def signal(sem, peer):
        pl.semaphore_signal(sem, inc=1, device_id=ident(peer), device_id_type=MESH)

    def later(peer):
        return (peer[1] > iz) | ((peer[1] == iz) & (peer[0] > ix))

    def lanes(b):
        return pl.ds(pl.multiple_of(b * LANES, LANES), LANES)

    loads = [
        pltpu.make_async_copy(x_hbm, xe.at[pl.ds(ROWS, ROWS)], load_sem.at[0]),
        pltpu.make_async_copy(up_hbm, upv, load_sem.at[1]),
        pltpu.make_async_copy(med_hbm, med_ref, load_sem.at[2]),
        pltpu.make_async_copy(short_hbm, short_ref, load_sem.at[3]),
    ]
    for copy in loads:
        copy.start()

    routes = [(at(1), at(-1)), (at(-1), at(1)), (at_x(1), at_x(-1)), (at_x(-1), at_x(1))]
    routes += [(at_z(d), at_z(-d)) for d in RAW + WIDE]
    barrier = pltpu.get_barrier_semaphore()
    known = jnp.int32(0)
    for peers in routes:
        for peer in peers:
            pl.when(later(peer))(functools.partial(signal, barrier, peer))
            known = known + jnp.where(later(peer), 0, 1)

    @pl.when(known > 0)
    def _():
        pl.semaphore_wait(barrier, known)

    for k, (_, source) in enumerate(routes):
        pl.when(jnp.logical_not(later(source)))(functools.partial(signal, go.at[k], source))

    def ready(k):
        @pl.when(later(routes[k][0]))
        def _():
            pl.semaphore_wait(go.at[k], 1)

    def halo(b):
        return pltpu.make_async_remote_copy(
            src_ref=xe.at[pl.ds(ROWS, ROWS), lanes(b)],
            dst_ref=xe.at[pl.ds(0, ROWS), lanes(b)],
            send_sem=halo_send.at[b],
            recv_sem=halo_recv.at[b],
            device_id=ident(at(1)),
            device_id_type=MESH,
        )

    follows = later(at(1))
    loads[0].wait()

    @pl.when((me < n - 1) & jnp.logical_not(follows))
    def _():
        for b in range(blocks):
            halo(b).start()

    loads[2].wait()
    loads[3].wait()

    rows2 = lax.broadcasted_iota(jnp.int32, (ROWS, LANES), 0)
    cols2 = lax.broadcasted_iota(jnp.int32, (ROWS, LANES), 1)
    lane_group = cols2 // GROUP

    flip = (rows2 + cols2 == LANES - 1).astype(BF16)
    mrev[...] = jnp.dot(med_ref[...], flip, preferred_element_type=F32)
    mfwd[...] = med_ref[...].astype(F32)
    chan = lax.broadcasted_iota(jnp.int32, (groups, width), 1) // GROUP
    own = lax.broadcasted_iota(jnp.int32, (groups, width), 0)
    spread = (chan == own).astype(BF16)
    sch[0:taps, :] = jnp.dot(short_ref[...], spread, preferred_element_type=F32)

    above = (cols2 > rows2).astype(F32).astype(BF16)
    below = (cols2 <= rows2).astype(F32).astype(BF16)

    def forward_table(b, carry):
        for k in range(PER):
            g = b * PER + k
            row = jnp.broadcast_to(mrev[pl.ds(g, 1), :], (ROWS, LANES))
            turned = pltpu.roll(row, 1, 1, stride=1, stride_axis=0).astype(BF16)
            top = pl.ds(pl.multiple_of(g * ROWS, ROWS), ROWS)
            tf[top, 0:LANES] = turned * above
            tf[top, LANES:] = turned * below
        return carry

    def next_halo():
        ready(0)

        @pl.when((me < n - 1) & follows)
        def _():
            for b in range(blocks):
                halo(b).start()

    lax.fori_loop(0, 1, forward_table, 0)
    next_halo()
    lax.fori_loop(1, blocks, forward_table, 0)
    ready(2)
    ready(3)
    for d in (1, -1):
        signal(across, at_x(d))

    big_r = lax.broadcasted_iota(jnp.int32, (2 * ROWS, 2 * ROWS), 0)
    big_c = lax.broadcasted_iota(jnp.int32, (2 * ROWS, 2 * ROWS), 1)
    flip_rows = (big_r + big_c == 2 * ROWS - 1).astype(BF16)

    loads[1].wait()

    def block(b, carry):
        @pl.when(me > 0)
        def _():
            halo(b).wait_recv()

        @pl.when(me == 0)
        def _():
            xe[pl.ds(0, ROWS), lanes(b)] = jnp.zeros((ROWS, LANES), BF16)

        xb = xe[:, lanes(b)]
        xf[...] = xe[pl.ds(ROWS - 16, ROWS + 16), lanes(b)].astype(F32)
        gate = jnp.zeros((ROWS, LANES), F32)
        for j in range(taps):
            gate = gate + sch[j : j + 1, lanes(b)] * xf[16 - j : 16 - j + ROWS, :]
        conv = jnp.zeros((ROWS, LANES), F32)
        for k in range(PER):
            top = pl.ds(pl.multiple_of((b * PER + k) * ROWS, ROWS), ROWS)
            term = jnp.dot(tf[top, :], xb, preferred_element_type=F32)
            conv = jnp.where(lane_group == k, term, conv)
        up = upv[:, lanes(b)].astype(F32)
        gate_cot = (up * conv).astype(BF16)
        conv_cot = (up * gate).astype(BF16)
        cce[0:ROWS, lanes(b)] = conv_cot
        gce[0:ROWS, lanes(b)] = gate_cot
        gate_f = gate_cot.astype(F32)
        for j in range(taps):
            sacc[j : j + 1, lanes(b)] = jnp.sum(
                gate_f * xf[16 - j : 16 - j + ROWS, :], axis=0, keepdims=True
            )
        x_rev = jnp.dot(flip_rows, xb, preferred_element_type=F32).astype(BF16)
        for k in range(PER):
            part = jnp.where(lane_group == k, conv_cot, jnp.zeros((), BF16))
            pair = nt(part, x_rev)
            both = jnp.where(rows2 + cols2 >= LANES - 1, pair[:, :LANES], pair[:, LANES:])
            turned = pltpu.roll(both, 1, 1, stride=1, stride_axis=0)
            rx[ix, pl.ds(b * PER + k, 1), :] = jnp.sum(turned, axis=0, keepdims=True)
        return carry

    sacc[...] = jnp.zeros_like(sacc)
    lax.fori_loop(0, blocks, block, 0)

    tall_r = lax.broadcasted_iota(jnp.int32, (width, LANES), 0) // GROUP
    tall_c = lax.broadcasted_iota(jnp.int32, (width, LANES), 1)
    rx[ix, groups : groups + 8, :] = jnp.dot(
        sacc[...],
        (tall_r == tall_c).astype(F32),
        preferred_element_type=F32,
        precision=lax.Precision.HIGHEST,
    )

    def remote(src, dst, send, recv, peer):
        return pltpu.make_async_remote_copy(
            src_ref=src, dst_ref=dst, send_sem=send, recv_sem=recv, device_id=ident(peer), device_id_type=MESH
        )

    pl.semaphore_wait(across, 2)
    x_sends = [
        remote(rx.at[ix], rx.at[ix], x_send.at[d - 1], x_recv.at[d - 1], at_x(d)) for d in (2, 1, 3)
    ]
    for copy in x_sends:
        copy.start()

    back_c = remote(
        cce.at[pl.ds(0, ROWS)], cce.at[pl.ds(ROWS, ROWS)], back_send.at[0], back_recv.at[0], at(-1)
    )
    back_g = remote(
        gce.at[pl.ds(0, 16)], gce.at[pl.ds(ROWS, 16)], back_send.at[1], back_recv.at[1], at(-1)
    )

    ready(1)

    @pl.when(me > 0)
    def _():
        back_g.start()
        back_c.start()

    strict = (cols2 < rows2).astype(F32).astype(BF16)
    upper = (cols2 >= rows2).astype(F32).astype(BF16)

    def backward_table(b, carry):
        for k in range(PER):
            g = b * PER + k
            row = jnp.broadcast_to(mfwd[pl.ds(g, 1), :], (ROWS, LANES))
            turned = pltpu.roll(row, 0, 1, stride=1, stride_axis=0).astype(BF16)
            top = pl.ds(pl.multiple_of(g * ROWS, ROWS), ROWS)
            tb[top, 0:LANES] = turned * upper
            tb[top, LANES:] = turned * strict
        return carry

    lax.fori_loop(0, blocks, backward_table, 0)

    for d in range(1, nx):
        source = lax.rem(ix - d + nx, nx)
        remote(rx.at[ix], rx.at[source], x_send.at[d - 1], x_recv.at[d - 1], at_x(d)).wait_recv()
    total = rx[0]
    for k in range(1, nx):
        total = total + rx[k]
    xs[...] = total.astype(BF16)
    z_sends = [remote(xs, rz.at[k], z_send.at[k], z_recv.at[k], at_z(d)) for k, d in enumerate(RAW)]
    for k, copy in enumerate(z_sends):
        ready(4 + k)
        copy.start()
    for copy in z_sends:
        copy.wait_recv()
    window = (total + rz[0].astype(F32)) + (rz[1].astype(F32) + rz[2].astype(F32))
    win[...] = window.astype(BF16)
    tot_ref[...] = window
    w_sends = [remote(win, rw.at[k], w_send.at[k], w_recv.at[k], at_z(d)) for k, d in enumerate(WIDE)]
    for k, copy in enumerate(w_sends):
        ready(4 + len(RAW) + k)
        copy.start()

    @pl.when(me < n - 1)
    def _():
        back_g.wait_recv()
        back_c.wait_recv()

    @pl.when(me == n - 1)
    def _():
        cce[pl.ds(ROWS, ROWS), :] = jnp.zeros((ROWS, width), BF16)
        gce[pl.ds(ROWS, 16), :] = jnp.zeros((16, width), BF16)

    def gradient(b, carry):
        cb = cce[:, lanes(b)]
        back = jnp.zeros((ROWS, LANES), F32)
        for k in range(PER):
            top = pl.ds(pl.multiple_of((b * PER + k) * ROWS, ROWS), ROWS)
            term = jnp.dot(tb[top, :], cb, preferred_element_type=F32)
            back = jnp.where(lane_group == k, term, back)
        xf[...] = gce[:, lanes(b)].astype(F32)
        short = jnp.zeros((ROWS, LANES), F32)
        for j in range(taps):
            short = short + sch[j : j + 1, lanes(b)] * xf[j : j + ROWS, :]
        igv[:, lanes(b)] = (back + short).astype(BF16)
        return carry

    lax.fori_loop(0, blocks, gradient, 0)

    for copy in w_sends:
        copy.wait_recv()
    tot_ref[...] = (tot_ref[...] + rw[0].astype(F32)) + (rw[1].astype(F32) + rw[2].astype(F32))

    @pl.when(me < n - 1)
    def _():
        for b in range(blocks):
            halo(b).wait_send()

    @pl.when(me > 0)
    def _():
        back_g.wait_send()
        back_c.wait_send()

    for copy in x_sends + z_sends + w_sends:
        copy.wait_send()


def finish(factor, ig_ref, tot_ref, ig_hbm, med_hbm, short_hbm, med_v, short_v, sems):
    groups, taps = med_v.shape[0], short_v.shape[0]
    big = pltpu.make_async_copy(ig_ref, ig_hbm, sems.at[0])
    big.start()
    med_v[...] = tot_ref[0:groups, :] * factor
    medium = pltpu.make_async_copy(med_v, med_hbm, sems.at[1])
    medium.start()
    short_v[...] = tot_ref[groups : groups + taps, 0:groups] * factor
    short = pltpu.make_async_copy(short_v, short_hbm, sems.at[2])
    short.start()
    big.wait()
    medium.wait()
    short.wait()


def local(nx, nz, inputs, upstream, medium_filter, short_filter):
    rows, width = inputs.shape
    groups, taps = medium_filter.shape
    short_taps = short_filter.shape[1]
    if rows != ROWS or taps != LANES or width % LANES or groups != 32:
        raise ValueError("unsupported sizes")
    height = groups + 8
    blocks = width // LANES
    vmem = pltpu.VMEM
    dma = pltpu.SemaphoreType.DMA
    hbm = pl.BlockSpec(memory_space=pl.ANY)
    local_mem = pl.BlockSpec(memory_space=pltpu.VMEM)
    gradient, total = pl.pallas_call(
        functools.partial(kernel, nx, nz),
        out_shape=(vmem((rows, width), BF16), vmem((height, LANES), F32)),
        in_specs=[hbm] * 4,
        out_specs=(local_mem, local_mem),
        scratch_shapes=[
            vmem((2 * ROWS, width), BF16),
            vmem((ROWS, width), BF16),
            vmem((groups, LANES), BF16),
            vmem((short_taps, groups), BF16),
            vmem((2 * ROWS, width), BF16),
            vmem((ROWS + 16, width), BF16),
            vmem((groups * ROWS, 2 * LANES), BF16),
            vmem((groups * ROWS, 2 * LANES), BF16),
            vmem((groups, LANES), F32),
            vmem((groups, LANES), F32),
            vmem((8, width), F32),
            vmem((ROWS + 16, LANES), F32),
            vmem((8, width), F32),
            vmem((nx, height, LANES), F32),
            vmem((height, LANES), BF16),
            vmem((len(RAW), height, LANES), BF16),
            vmem((height, LANES), BF16),
            vmem((len(WIDE), height, LANES), BF16),
            dma((4,)),
            dma((blocks,)),
            dma((blocks,)),
            dma((2,)),
            dma((2,)),
            dma((nx - 1,)),
            dma((nx - 1,)),
            dma((len(RAW),)),
            dma((len(RAW),)),
            dma((len(WIDE),)),
            dma((len(WIDE),)),
            pltpu.SemaphoreType.REGULAR((4 + len(RAW) + len(WIDE),)),
            pltpu.SemaphoreType.REGULAR,
        ],
        compiler_params=pltpu.CompilerParams(collective_id=0, has_side_effects=True),
    )(inputs, upstream, medium_filter, short_filter.T)
    factor = float(GROUP * rows * lax.axis_size("ctx")) ** (-0.5)
    gradient, medium, short = pl.pallas_call(
        functools.partial(finish, factor),
        out_shape=(
            jax.ShapeDtypeStruct((rows, width), BF16),
            jax.ShapeDtypeStruct((groups, LANES), F32),
            jax.ShapeDtypeStruct((short_taps, groups), F32),
        ),
        in_specs=[local_mem, local_mem],
        out_specs=(hbm, hbm, hbm),
        scratch_shapes=[vmem((groups, LANES), F32), vmem((short_taps, groups), F32), dma((3,))],
    )(pltpu.with_memory_space_constraint(gradient, pltpu.VMEM), pltpu.with_memory_space_constraint(total, pltpu.VMEM))
    return gradient, medium, short.T


def solution(mesh):
    n = mesh.shape["ctx"]
    nz = 16
    return jax.shard_map(
        functools.partial(local, n // nz, nz),
        mesh=mesh,
        in_specs=(P("ctx", "fsdp"), P("ctx", "fsdp"), P("fsdp", None), P("fsdp", None)),
        out_specs=(P("ctx", "fsdp"), P("fsdp", None), P("fsdp", None)),
        check_vma=False,
    )
```

```python
import functools

import jax
import jax.numpy as jnp
from jax import lax
from jax.experimental import pallas as pl
from jax.experimental.pallas import tpu as pltpu
from jax.sharding import PartitionSpec as P

GROUP = 16
ROWS = 128
LANES = 128
PER = LANES // GROUP
MESH = pl.DeviceIdType.MESH
RAW = (1, 2, 3)
WIDE = (4, -4, 8)
F32 = jnp.float32
BF16 = jnp.bfloat16


def nt(a, b):
    return lax.dot_general(a, b, (((1,), (1,)), ((), ())), preferred_element_type=F32)


def kernel(
    nx, nz, x_hbm, up_hbm, med_hbm, short_hbm, igv, tot_ref,
    xe, upv, med_ref, short_ref, cce, gce, tf, tb, mrev, mfwd, sch, xf, sacc,
    rx, xs, rz, win, rw,
    load_sem, halo_send, halo_recv, back_send, back_recv,
    x_send, x_recv, z_send, z_recv, w_send, w_recv, go, steps,
):
    n = nx * nz
    width = xe.shape[1]
    blocks = width // LANES
    groups = width // GROUP
    taps = short_ref.shape[0]
    me = lax.axis_index("ctx")
    ix, iz = me // nz, lax.rem(me, nz)

    def at_z(d):
        return ix, lax.rem(iz + d + nz, nz)

    def at_x(d):
        return lax.rem(ix + d + nx, nx), iz

    def at(d):
        other = lax.rem(me + d + n, n)
        return other // nz, lax.rem(other, nz)

    def ident(peer):
        return {"ctx": peer[0] * nz + peer[1]}

    def signal(sem, peer):
        pl.semaphore_signal(sem, inc=1, device_id=ident(peer), device_id_type=MESH)

    def lanes(b):
        return pl.ds(pl.multiple_of(b * LANES, LANES), LANES)

    loads = [
        pltpu.make_async_copy(x_hbm, xe.at[pl.ds(ROWS, ROWS)], load_sem.at[0]),
        pltpu.make_async_copy(up_hbm, upv, load_sem.at[1]),
        pltpu.make_async_copy(med_hbm, med_ref, load_sem.at[2]),
        pltpu.make_async_copy(short_hbm, short_ref, load_sem.at[3]),
    ]
    for copy in loads:
        copy.start()

    barrier = pltpu.get_barrier_semaphore()
    for peer in (at(-1), at_x(1), at_x(-1)):
        signal(barrier, peer)

    def halo(b):
        return pltpu.make_async_remote_copy(
            src_ref=xe.at[pl.ds(ROWS, ROWS), lanes(b)],
            dst_ref=xe.at[pl.ds(0, ROWS), lanes(b)],
            send_sem=halo_send.at[b],
            recv_sem=halo_recv.at[b],
            device_id=ident(at(1)),
            device_id_type=MESH,
        )

    loads[2].wait()
    loads[3].wait()

    rows2 = lax.broadcasted_iota(jnp.int32, (ROWS, LANES), 0)
    cols2 = lax.broadcasted_iota(jnp.int32, (ROWS, LANES), 1)
    lane_group = cols2 // GROUP

    flip = (rows2 + cols2 == LANES - 1).astype(BF16)
    mrev[...] = jnp.dot(med_ref[...], flip, preferred_element_type=F32)
    mfwd[...] = med_ref[...].astype(F32)
    chan = lax.broadcasted_iota(jnp.int32, (groups, width), 1) // GROUP
    own = lax.broadcasted_iota(jnp.int32, (groups, width), 0)
    spread = (chan == own).astype(BF16)
    sch[0:taps, :] = jnp.dot(short_ref[...], spread, preferred_element_type=F32)

    above = (cols2 > rows2).astype(F32).astype(BF16)
    below = (cols2 <= rows2).astype(F32).astype(BF16)

    def forward_table(b, carry):
        for k in range(PER):
            g = b * PER + k
            row = jnp.broadcast_to(mrev[pl.ds(g, 1), :], (ROWS, LANES))
            turned = pltpu.roll(row, 1, 1, stride=1, stride_axis=0).astype(BF16)
            top = pl.ds(pl.multiple_of(g * ROWS, ROWS), ROWS)
            tf[top, 0:LANES] = turned * above
            tf[top, LANES:] = turned * below
        return carry

    def tell_sides():
        for d in (1, -1):
            signal(steps.at[0], at_x(d))

    def tell_next():
        signal(steps.at[1], at_z(-1))
        signal(steps.at[2], at_z(1))

    edge = (iz == 0) | (iz == nz - 1)

    lax.fori_loop(0, 1, forward_table, 0)
    loads[0].wait()
    pl.semaphore_wait(barrier, 3)

    @pl.when(me < n - 1)
    def _():
        for b in range(blocks):
            halo(b).start()

    @pl.when(me == n - 1)
    def _():
        signal(go, at(1))

    @pl.when(me == 0)
    def _():
        pl.semaphore_wait(go, 1)

    lax.fori_loop(1, blocks, forward_table, 0)

    big_r = lax.broadcasted_iota(jnp.int32, (2 * ROWS, 2 * ROWS), 0)
    big_c = lax.broadcasted_iota(jnp.int32, (2 * ROWS, 2 * ROWS), 1)
    flip_rows = (big_r + big_c == 2 * ROWS - 1).astype(BF16)

    loads[1].wait()

    def block(b, carry):
        @pl.when(me > 0)
        def _():
            halo(b).wait_recv()

        @pl.when(me == 0)
        def _():
            xe[pl.ds(0, ROWS), lanes(b)] = jnp.zeros((ROWS, LANES), BF16)

        xb = xe[:, lanes(b)]
        xf[...] = xe[pl.ds(ROWS - 16, ROWS + 16), lanes(b)].astype(F32)
        gate = jnp.zeros((ROWS, LANES), F32)
        for j in range(taps):
            gate = gate + sch[j : j + 1, lanes(b)] * xf[16 - j : 16 - j + ROWS, :]
        conv = jnp.zeros((ROWS, LANES), F32)
        for k in range(PER):
            top = pl.ds(pl.multiple_of((b * PER + k) * ROWS, ROWS), ROWS)
            term = jnp.dot(tf[top, :], xb, preferred_element_type=F32)
            conv = jnp.where(lane_group == k, term, conv)
        up = upv[:, lanes(b)].astype(F32)
        gate_cot = (up * conv).astype(BF16)
        conv_cot = (up * gate).astype(BF16)
        cce[0:ROWS, lanes(b)] = conv_cot
        gce[0:ROWS, lanes(b)] = gate_cot
        gate_f = gate_cot.astype(F32)
        for j in range(taps):
            sacc[j : j + 1, lanes(b)] = jnp.sum(
                gate_f * xf[16 - j : 16 - j + ROWS, :], axis=0, keepdims=True
            )
        x_rev = jnp.dot(flip_rows, xb, preferred_element_type=F32).astype(BF16)
        for k in range(PER):
            part = jnp.where(lane_group == k, conv_cot, jnp.zeros((), BF16))
            pair = nt(part, x_rev)
            both = jnp.where(rows2 + cols2 >= LANES - 1, pair[:, :LANES], pair[:, LANES:])
            turned = pltpu.roll(both, 1, 1, stride=1, stride_axis=0)
            rx[ix, pl.ds(b * PER + k, 1), :] = jnp.sum(turned, axis=0, keepdims=True)
        @pl.when(b == 0)
        def _():
            tell_sides()
            pl.when(jnp.logical_not(edge))(tell_next)

        @pl.when(b == 2)
        def _():
            pl.semaphore_wait(steps.at[0], 2)
            pl.when(edge)(tell_next)

        return carry

    sacc[...] = jnp.zeros_like(sacc)
    lax.fori_loop(0, blocks, block, 0)

    tall_r = lax.broadcasted_iota(jnp.int32, (width, LANES), 0) // GROUP
    tall_c = lax.broadcasted_iota(jnp.int32, (width, LANES), 1)
    rx[ix, groups : groups + 8, :] = jnp.dot(
        sacc[...],
        (tall_r == tall_c).astype(F32),
        preferred_element_type=F32,
        precision=lax.Precision.HIGHEST,
    )

    def remote(src, dst, send, recv, peer):
        return pltpu.make_async_remote_copy(
            src_ref=src, dst_ref=dst, send_sem=send, recv_sem=recv, device_id=ident(peer), device_id_type=MESH
        )

    x_sends = [
        remote(rx.at[ix], rx.at[ix], x_send.at[d - 1], x_recv.at[d - 1], at_x(d)) for d in (2, 1, 3)
    ]
    for copy in x_sends:
        copy.start()
    back_c = remote(
        cce.at[pl.ds(0, ROWS)], cce.at[pl.ds(ROWS, ROWS)], back_send.at[0], back_recv.at[0], at(-1)
    )
    back_g = remote(
        gce.at[pl.ds(0, 16)], gce.at[pl.ds(ROWS, 16)], back_send.at[1], back_recv.at[1], at(-1)
    )

    @pl.when(me > 0)
    def _():
        back_g.start()
        back_c.start()

    strict = (cols2 < rows2).astype(F32).astype(BF16)
    upper = (cols2 >= rows2).astype(F32).astype(BF16)

    def backward_table(b, carry):
        for k in range(PER):
            g = b * PER + k
            row = jnp.broadcast_to(mfwd[pl.ds(g, 1), :], (ROWS, LANES))
            turned = pltpu.roll(row, 0, 1, stride=1, stride_axis=0).astype(BF16)
            top = pl.ds(pl.multiple_of(g * ROWS, ROWS), ROWS)
            tb[top, 0:LANES] = turned * upper
            tb[top, LANES:] = turned * strict
        return carry

    pl.semaphore_wait(steps.at[1], 1)
    lax.fori_loop(0, blocks, backward_table, 0)
    pl.semaphore_wait(steps.at[2], 1)
    signal(steps.at[3], at_z(-2))
    signal(steps.at[4], at_z(2))

    for d in range(1, nx):
        source = lax.rem(ix - d + nx, nx)
        remote(rx.at[ix], rx.at[source], x_send.at[d - 1], x_recv.at[d - 1], at_x(d)).wait_recv()
    total = rx[0]
    for k in range(1, nx):
        total = total + rx[k]
    xs[...] = total.astype(BF16)
    z_sends = [remote(xs, rz.at[k], z_send.at[k], z_recv.at[k], at_z(d)) for k, d in enumerate(RAW)]
    z_sends[0].start()
    z_sends[1].start()
    pl.semaphore_wait(steps.at[3], 1)
    z_sends[2].start()
    pl.semaphore_wait(steps.at[4], 1)
    signal(steps.at[5], at_z(4))
    for copy in z_sends:
        copy.wait_recv()
    window = (total + rz[0].astype(F32)) + (rz[1].astype(F32) + rz[2].astype(F32))
    win[...] = window.astype(BF16)
    tot_ref[...] = window
    w_sends = [remote(win, rw.at[k], w_send.at[k], w_recv.at[k], at_z(d)) for k, d in enumerate(WIDE)]
    for copy in w_sends[:2]:
        copy.start()
    pl.semaphore_wait(steps.at[5], 1)
    w_sends[2].start()

    @pl.when(me < n - 1)
    def _():
        back_g.wait_recv()
        back_c.wait_recv()

    @pl.when(me == n - 1)
    def _():
        cce[pl.ds(ROWS, ROWS), :] = jnp.zeros((ROWS, width), BF16)
        gce[pl.ds(ROWS, 16), :] = jnp.zeros((16, width), BF16)

    def gradient(b, carry):
        cb = cce[:, lanes(b)]
        back = jnp.zeros((ROWS, LANES), F32)
        for k in range(PER):
            top = pl.ds(pl.multiple_of((b * PER + k) * ROWS, ROWS), ROWS)
            term = jnp.dot(tb[top, :], cb, preferred_element_type=F32)
            back = jnp.where(lane_group == k, term, back)
        xf[...] = gce[:, lanes(b)].astype(F32)
        short = jnp.zeros((ROWS, LANES), F32)
        for j in range(taps):
            short = short + sch[j : j + 1, lanes(b)] * xf[j : j + ROWS, :]
        igv[:, lanes(b)] = (back + short).astype(BF16)
        return carry

    lax.fori_loop(0, blocks, gradient, 0)

    for copy in w_sends:
        copy.wait_recv()
    tot_ref[...] = (tot_ref[...] + rw[0].astype(F32)) + (rw[1].astype(F32) + rw[2].astype(F32))

    @pl.when(me < n - 1)
    def _():
        for b in range(blocks):
            halo(b).wait_send()

    @pl.when(me > 0)
    def _():
        back_g.wait_send()
        back_c.wait_send()

    for copy in x_sends + z_sends + w_sends:
        copy.wait_send()


def finish(factor, ig_ref, tot_ref, ig_hbm, med_hbm, short_hbm, med_v, short_v, sems):
    groups, taps = med_v.shape[0], short_v.shape[0]
    big = pltpu.make_async_copy(ig_ref, ig_hbm, sems.at[0])
    big.start()
    med_v[...] = tot_ref[0:groups, :] * factor
    medium = pltpu.make_async_copy(med_v, med_hbm, sems.at[1])
    medium.start()
    short_v[...] = tot_ref[groups : groups + taps, 0:groups] * factor
    short = pltpu.make_async_copy(short_v, short_hbm, sems.at[2])
    short.start()
    big.wait()
    medium.wait()
    short.wait()


def local(nx, nz, inputs, upstream, medium_filter, short_filter):
    rows, width = inputs.shape
    groups, taps = medium_filter.shape
    short_taps = short_filter.shape[1]
    if rows != ROWS or taps != LANES or width % LANES or groups != 32:
        raise ValueError("unsupported sizes")
    height = groups + 8
    blocks = width // LANES
    vmem = pltpu.VMEM
    dma = pltpu.SemaphoreType.DMA
    hbm = pl.BlockSpec(memory_space=pl.ANY)
    local_mem = pl.BlockSpec(memory_space=pltpu.VMEM)
    gradient, total = pl.pallas_call(
        functools.partial(kernel, nx, nz),
        out_shape=(vmem((rows, width), BF16), vmem((height, LANES), F32)),
        in_specs=[hbm] * 4,
        out_specs=(local_mem, local_mem),
        scratch_shapes=[
            vmem((2 * ROWS, width), BF16),
            vmem((ROWS, width), BF16),
            vmem((groups, LANES), BF16),
            vmem((short_taps, groups), BF16),
            vmem((2 * ROWS, width), BF16),
            vmem((ROWS + 16, width), BF16),
            vmem((groups * ROWS, 2 * LANES), BF16),
            vmem((groups * ROWS, 2 * LANES), BF16),
            vmem((groups, LANES), F32),
            vmem((groups, LANES), F32),
            vmem((8, width), F32),
            vmem((ROWS + 16, LANES), F32),
            vmem((8, width), F32),
            vmem((nx, height, LANES), F32),
            vmem((height, LANES), BF16),
            vmem((len(RAW), height, LANES), BF16),
            vmem((height, LANES), BF16),
            vmem((len(WIDE), height, LANES), BF16),
            dma((4,)),
            dma((blocks,)),
            dma((blocks,)),
            dma((2,)),
            dma((2,)),
            dma((nx - 1,)),
            dma((nx - 1,)),
            dma((len(RAW),)),
            dma((len(RAW),)),
            dma((len(WIDE),)),
            dma((len(WIDE),)),
            pltpu.SemaphoreType.REGULAR,
            pltpu.SemaphoreType.REGULAR((6,)),
        ],
        compiler_params=pltpu.CompilerParams(collective_id=0, has_side_effects=True),
    )(inputs, upstream, medium_filter, short_filter.T)
    factor = float(GROUP * rows * lax.axis_size("ctx")) ** (-0.5)
    gradient, medium, short = pl.pallas_call(
        functools.partial(finish, factor),
        out_shape=(
            jax.ShapeDtypeStruct((rows, width), BF16),
            jax.ShapeDtypeStruct((groups, LANES), F32),
            jax.ShapeDtypeStruct((short_taps, groups), F32),
        ),
        in_specs=[local_mem, local_mem],
        out_specs=(hbm, hbm, hbm),
        scratch_shapes=[vmem((groups, LANES), F32), vmem((short_taps, groups), F32), dma((3,))],
    )(pltpu.with_memory_space_constraint(gradient, pltpu.VMEM), pltpu.with_memory_space_constraint(total, pltpu.VMEM))
    return gradient, medium, short.T


def solution(mesh):
    n = mesh.shape["ctx"]
    nz = 16
    return jax.shard_map(
        functools.partial(local, n // nz, nz),
        mesh=mesh,
        in_specs=(P("ctx", "fsdp"), P("ctx", "fsdp"), P("fsdp", None), P("fsdp", None)),
        out_specs=(P("ctx", "fsdp"), P("fsdp", None), P("fsdp", None)),
        check_vma=False,
    )
```

```python
import functools

import jax
import jax.numpy as jnp
from jax import lax
from jax.experimental import pallas as pl
from jax.experimental.pallas import tpu as pltpu
from jax.sharding import PartitionSpec as P

GROUP = 16
ROWS = 128
LANES = 128
PER = LANES // GROUP
MESH = pl.DeviceIdType.MESH
RAW = (1, 2, 3)
WIDE = (4, -4, 8)
F32 = jnp.float32
BF16 = jnp.bfloat16


def nt(a, b):
    return lax.dot_general(a, b, (((1,), (1,)), ((), ())), preferred_element_type=F32)


def kernel(
    nx, nz, x_hbm, up_hbm, med_hbm, short_hbm, igv, tot_ref,
    xe, upv, med_ref, short_ref, cce, gce, tf, tb, mrev, mfwd, sch, xf, sacc, pick,
    rx, xs, rz, win, rw,
    load_sem, halo_send, halo_recv, back_send, back_recv,
    x_send, x_recv, z_send, z_recv, w_send, w_recv, go, steps,
):
    n = nx * nz
    width = xe.shape[1]
    blocks = width // LANES
    groups = width // GROUP
    taps = short_ref.shape[0]
    me = lax.axis_index("ctx")
    ix, iz = me // nz, lax.rem(me, nz)

    def at_z(d):
        return ix, lax.rem(iz + d + nz, nz)

    def at_x(d):
        return lax.rem(ix + d + nx, nx), iz

    def at(d):
        other = lax.rem(me + d + n, n)
        return other // nz, lax.rem(other, nz)

    def ident(peer):
        return {"ctx": peer[0] * nz + peer[1]}

    def signal(sem, peer):
        pl.semaphore_signal(sem, inc=1, device_id=ident(peer), device_id_type=MESH)

    def lanes(b):
        return pl.ds(pl.multiple_of(b * LANES, LANES), LANES)

    loads = [
        pltpu.make_async_copy(x_hbm, xe.at[pl.ds(ROWS, ROWS)], load_sem.at[0]),
        pltpu.make_async_copy(up_hbm, upv, load_sem.at[1]),
        pltpu.make_async_copy(med_hbm, med_ref, load_sem.at[2]),
        pltpu.make_async_copy(short_hbm, short_ref, load_sem.at[3]),
    ]
    for copy in loads:
        copy.start()

    barrier = pltpu.get_barrier_semaphore()
    for peer in (at(-1), at_x(1), at_x(-1)):
        signal(barrier, peer)

    def halo(b):
        return pltpu.make_async_remote_copy(
            src_ref=xe.at[pl.ds(ROWS, ROWS), lanes(b)],
            dst_ref=xe.at[pl.ds(0, ROWS), lanes(b)],
            send_sem=halo_send.at[b],
            recv_sem=halo_recv.at[b],
            device_id=ident(at(1)),
            device_id_type=MESH,
        )

    loads[0].wait()
    pl.semaphore_wait(barrier, 3)

    @pl.when(me < n - 1)
    def _():
        for b in range(blocks):
            halo(b).start()

    @pl.when(me == n - 1)
    def _():
        signal(go, at(1))

    loads[2].wait()
    loads[3].wait()

    rows2 = lax.broadcasted_iota(jnp.int32, (ROWS, LANES), 0)
    cols2 = lax.broadcasted_iota(jnp.int32, (ROWS, LANES), 1)
    lane_group = cols2 // GROUP

    flip = (rows2 + cols2 == LANES - 1).astype(BF16)
    mrev[...] = jnp.dot(med_ref[...], flip, preferred_element_type=F32)
    mfwd[...] = med_ref[...].astype(F32)
    chan = lax.broadcasted_iota(jnp.int32, (groups, width), 1) // GROUP
    own = lax.broadcasted_iota(jnp.int32, (groups, width), 0)
    spread = (chan == own).astype(BF16)
    sch[0:taps, :] = jnp.dot(short_ref[...], spread, preferred_element_type=F32)

    above = (cols2 > rows2).astype(F32).astype(BF16)
    below = (cols2 <= rows2).astype(F32).astype(BF16)

    def forward_table(b, carry):
        for k in range(PER):
            g = b * PER + k
            row = jnp.broadcast_to(mrev[pl.ds(g, 1), :], (ROWS, LANES))
            turned = pltpu.roll(row, 1, 1, stride=1, stride_axis=0).astype(BF16)
            top = pl.ds(pl.multiple_of(g * ROWS, ROWS), ROWS)
            tf[top, 0:LANES] = turned * above
            tf[top, LANES:] = turned * below
        return carry

    def tell_sides():
        for d in (1, -1):
            signal(steps.at[0], at_x(d))

    def tell_next():
        signal(steps.at[1], at_z(-1))
        signal(steps.at[2], at_z(1))

    edge = (iz == 0) | (iz == nz - 1)

    lax.fori_loop(0, blocks, forward_table, 0)

    @pl.when(me == 0)
    def _():
        pl.semaphore_wait(go, 1)

    tall_r = lax.broadcasted_iota(jnp.int32, (width, LANES), 0) // GROUP
    tall_c = lax.broadcasted_iota(jnp.int32, (width, LANES), 1)
    pick[...] = (tall_r == tall_c).astype(BF16)

    big_r = lax.broadcasted_iota(jnp.int32, (2 * ROWS, 2 * ROWS), 0)
    big_c = lax.broadcasted_iota(jnp.int32, (2 * ROWS, 2 * ROWS), 1)
    flip_rows = (big_r + big_c == 2 * ROWS - 1).astype(BF16)

    loads[1].wait()

    def block(b, carry):
        @pl.when(me > 0)
        def _():
            halo(b).wait_recv()

        @pl.when(me == 0)
        def _():
            xe[pl.ds(0, ROWS), lanes(b)] = jnp.zeros((ROWS, LANES), BF16)

        xb = xe[:, lanes(b)]
        xf[...] = xe[pl.ds(ROWS - 16, ROWS + 16), lanes(b)].astype(F32)
        gate = jnp.zeros((ROWS, LANES), F32)
        for j in range(taps):
            gate = gate + sch[j : j + 1, lanes(b)] * xf[16 - j : 16 - j + ROWS, :]
        conv = jnp.zeros((ROWS, LANES), F32)
        for k in range(PER):
            top = pl.ds(pl.multiple_of((b * PER + k) * ROWS, ROWS), ROWS)
            term = jnp.dot(tf[top, :], xb, preferred_element_type=F32)
            conv = jnp.where(lane_group == k, term, conv)
        up = upv[:, lanes(b)].astype(F32)
        gate_cot = (up * conv).astype(BF16)
        conv_cot = (up * gate).astype(BF16)
        cce[0:ROWS, lanes(b)] = conv_cot
        gce[0:ROWS, lanes(b)] = gate_cot
        gate_f = gate_cot.astype(F32)
        for j in range(taps):
            sacc[j : j + 1, lanes(b)] = jnp.sum(
                gate_f * xf[16 - j : 16 - j + ROWS, :], axis=0, keepdims=True
            )
        x_rev = jnp.dot(flip_rows, xb, preferred_element_type=F32).astype(BF16)
        for k in range(PER):
            part = jnp.where(lane_group == k, conv_cot, jnp.zeros((), BF16))
            pair = nt(part, x_rev)
            both = jnp.where(rows2 + cols2 >= LANES - 1, pair[:, :LANES], pair[:, LANES:])
            turned = pltpu.roll(both, 1, 1, stride=1, stride_axis=0)
            rx[ix, pl.ds(b * PER + k, 1), :] = jnp.sum(turned, axis=0, keepdims=True)
        @pl.when(b == 0)
        def _():
            tell_sides()
            pl.when(jnp.logical_not(edge))(tell_next)

        @pl.when(b == 2)
        def _():
            pl.semaphore_wait(steps.at[0], 2)
            pl.when(edge)(tell_next)

        return carry

    sacc[...] = jnp.zeros_like(sacc)
    lax.fori_loop(0, blocks, block, 0)

    sums = sacc[...]
    top = sums.astype(BF16)
    rest = sums - top.astype(F32)
    middle = rest.astype(BF16)
    low = (rest - middle.astype(F32)).astype(BF16)
    pieces = [jnp.dot(p, pick[...], preferred_element_type=F32) for p in (top, middle, low)]
    rx[ix, groups : groups + 8, :] = pieces[0] + (pieces[1] + pieces[2])

    def remote(src, dst, send, recv, peer):
        return pltpu.make_async_remote_copy(
            src_ref=src, dst_ref=dst, send_sem=send, recv_sem=recv, device_id=ident(peer), device_id_type=MESH
        )

    x_sends = [
        remote(rx.at[ix], rx.at[ix], x_send.at[d - 1], x_recv.at[d - 1], at_x(d)) for d in (2, 1, 3)
    ]
    for copy in x_sends:
        copy.start()
    back_c = remote(
        cce.at[pl.ds(0, ROWS)], cce.at[pl.ds(ROWS, ROWS)], back_send.at[0], back_recv.at[0], at(-1)
    )
    back_g = remote(
        gce.at[pl.ds(0, 16)], gce.at[pl.ds(ROWS, 16)], back_send.at[1], back_recv.at[1], at(-1)
    )

    @pl.when(me > 0)
    def _():
        back_g.start()
        back_c.start()

    strict = (cols2 < rows2).astype(F32).astype(BF16)
    upper = (cols2 >= rows2).astype(F32).astype(BF16)

    def backward_table(b, carry):
        for k in range(PER):
            g = b * PER + k
            row = jnp.broadcast_to(mfwd[pl.ds(g, 1), :], (ROWS, LANES))
            turned = pltpu.roll(row, 0, 1, stride=1, stride_axis=0).astype(BF16)
            top = pl.ds(pl.multiple_of(g * ROWS, ROWS), ROWS)
            tb[top, 0:LANES] = turned * upper
            tb[top, LANES:] = turned * strict
        return carry

    pl.semaphore_wait(steps.at[1], 1)
    lax.fori_loop(0, blocks, backward_table, 0)
    pl.semaphore_wait(steps.at[2], 1)
    signal(steps.at[3], at_z(-2))
    signal(steps.at[4], at_z(2))

    for d in range(1, nx):
        source = lax.rem(ix - d + nx, nx)
        remote(rx.at[ix], rx.at[source], x_send.at[d - 1], x_recv.at[d - 1], at_x(d)).wait_recv()
    total = rx[0]
    for k in range(1, nx):
        total = total + rx[k]
    xs[...] = total.astype(BF16)
    z_sends = [remote(xs, rz.at[k], z_send.at[k], z_recv.at[k], at_z(d)) for k, d in enumerate(RAW)]
    z_sends[0].start()
    z_sends[1].start()
    pl.semaphore_wait(steps.at[3], 1)
    z_sends[2].start()
    pl.semaphore_wait(steps.at[4], 1)
    signal(steps.at[5], at_z(4))
    for copy in z_sends:
        copy.wait_recv()
    window = (total + rz[0].astype(F32)) + (rz[1].astype(F32) + rz[2].astype(F32))
    win[...] = window.astype(BF16)
    tot_ref[...] = window
    w_sends = [remote(win, rw.at[k], w_send.at[k], w_recv.at[k], at_z(d)) for k, d in enumerate(WIDE)]
    for copy in w_sends[:2]:
        copy.start()
    pl.semaphore_wait(steps.at[5], 1)
    w_sends[2].start()

    @pl.when(me < n - 1)
    def _():
        back_g.wait_recv()
        back_c.wait_recv()

    @pl.when(me == n - 1)
    def _():
        cce[pl.ds(ROWS, ROWS), :] = jnp.zeros((ROWS, width), BF16)
        gce[pl.ds(ROWS, 16), :] = jnp.zeros((16, width), BF16)

    def gradient(b, carry):
        cb = cce[:, lanes(b)]
        back = jnp.zeros((ROWS, LANES), F32)
        for k in range(PER):
            top = pl.ds(pl.multiple_of((b * PER + k) * ROWS, ROWS), ROWS)
            term = jnp.dot(tb[top, :], cb, preferred_element_type=F32)
            back = jnp.where(lane_group == k, term, back)
        xf[...] = gce[:, lanes(b)].astype(F32)
        short = jnp.zeros((ROWS, LANES), F32)
        for j in range(taps):
            short = short + sch[j : j + 1, lanes(b)] * xf[j : j + ROWS, :]
        igv[:, lanes(b)] = (back + short).astype(BF16)
        return carry

    lax.fori_loop(0, blocks, gradient, 0)

    for copy in w_sends:
        copy.wait_recv()
    tot_ref[...] = (tot_ref[...] + rw[0].astype(F32)) + (rw[1].astype(F32) + rw[2].astype(F32))

    @pl.when(me < n - 1)
    def _():
        for b in range(blocks):
            halo(b).wait_send()

    @pl.when(me > 0)
    def _():
        back_g.wait_send()
        back_c.wait_send()

    for copy in x_sends + z_sends + w_sends:
        copy.wait_send()


def finish(factor, ig_ref, tot_ref, ig_hbm, med_hbm, short_hbm, med_v, short_v, sems):
    groups, taps = med_v.shape[0], short_v.shape[0]
    big = pltpu.make_async_copy(ig_ref, ig_hbm, sems.at[0])
    big.start()
    med_v[...] = tot_ref[0:groups, :] * factor
    medium = pltpu.make_async_copy(med_v, med_hbm, sems.at[1])
    medium.start()
    short_v[...] = tot_ref[groups : groups + taps, 0:groups] * factor
    short = pltpu.make_async_copy(short_v, short_hbm, sems.at[2])
    short.start()
    big.wait()
    medium.wait()
    short.wait()


def local(nx, nz, inputs, upstream, medium_filter, short_filter):
    rows, width = inputs.shape
    groups, taps = medium_filter.shape
    short_taps = short_filter.shape[1]
    if rows != ROWS or taps != LANES or width % LANES or groups != 32:
        raise ValueError("unsupported sizes")
    height = groups + 8
    blocks = width // LANES
    vmem = pltpu.VMEM
    dma = pltpu.SemaphoreType.DMA
    hbm = pl.BlockSpec(memory_space=pl.ANY)
    local_mem = pl.BlockSpec(memory_space=pltpu.VMEM)
    gradient, total = pl.pallas_call(
        functools.partial(kernel, nx, nz),
        out_shape=(vmem((rows, width), BF16), vmem((height, LANES), F32)),
        in_specs=[hbm] * 4,
        out_specs=(local_mem, local_mem),
        scratch_shapes=[
            vmem((2 * ROWS, width), BF16),
            vmem((ROWS, width), BF16),
            vmem((groups, LANES), BF16),
            vmem((short_taps, groups), BF16),
            vmem((2 * ROWS, width), BF16),
            vmem((ROWS + 16, width), BF16),
            vmem((groups * ROWS, 2 * LANES), BF16),
            vmem((groups * ROWS, 2 * LANES), BF16),
            vmem((groups, LANES), F32),
            vmem((groups, LANES), F32),
            vmem((8, width), F32),
            vmem((ROWS + 16, LANES), F32),
            vmem((8, width), F32),
            vmem((width, LANES), BF16),
            vmem((nx, height, LANES), F32),
            vmem((height, LANES), BF16),
            vmem((len(RAW), height, LANES), BF16),
            vmem((height, LANES), BF16),
            vmem((len(WIDE), height, LANES), BF16),
            dma((4,)),
            dma((blocks,)),
            dma((blocks,)),
            dma((2,)),
            dma((2,)),
            dma((nx - 1,)),
            dma((nx - 1,)),
            dma((len(RAW),)),
            dma((len(RAW),)),
            dma((len(WIDE),)),
            dma((len(WIDE),)),
            pltpu.SemaphoreType.REGULAR,
            pltpu.SemaphoreType.REGULAR((6,)),
        ],
        compiler_params=pltpu.CompilerParams(collective_id=0, has_side_effects=True),
    )(inputs, upstream, medium_filter, short_filter.T)
    factor = float(GROUP * rows * lax.axis_size("ctx")) ** (-0.5)
    gradient, medium, short = pl.pallas_call(
        functools.partial(finish, factor),
        out_shape=(
            jax.ShapeDtypeStruct((rows, width), BF16),
            jax.ShapeDtypeStruct((groups, LANES), F32),
            jax.ShapeDtypeStruct((short_taps, groups), F32),
        ),
        in_specs=[local_mem, local_mem],
        out_specs=(hbm, hbm, hbm),
        scratch_shapes=[vmem((groups, LANES), F32), vmem((short_taps, groups), F32), dma((3,))],
    )(pltpu.with_memory_space_constraint(gradient, pltpu.VMEM), pltpu.with_memory_space_constraint(total, pltpu.VMEM))
    return gradient, medium, short.T


def solution(mesh):
    n = mesh.shape["ctx"]
    nz = 16
    return jax.shard_map(
        functools.partial(local, n // nz, nz),
        mesh=mesh,
        in_specs=(P("ctx", "fsdp"), P("ctx", "fsdp"), P("fsdp", None), P("fsdp", None)),
        out_specs=(P("ctx", "fsdp"), P("fsdp", None), P("fsdp", None)),
        check_vma=False,
    )
```

```python
import functools

import jax
import jax.numpy as jnp
from jax import lax
from jax.experimental import pallas as pl
from jax.experimental.pallas import tpu as pltpu
from jax.sharding import PartitionSpec as P

GROUP = 16
ROWS = 128
LANES = 128
PER = LANES // GROUP
MESH = pl.DeviceIdType.MESH
RAW = (1, 2, 3)
WIDE = (4, -4, 8)
F32 = jnp.float32
BF16 = jnp.bfloat16


def nt(a, b):
    return lax.dot_general(a, b, (((1,), (1,)), ((), ())), preferred_element_type=F32)


def kernel(
    nx, nz, x_hbm, up_hbm, med_hbm, short_hbm, igv, tot_ref,
    xe, upv, med_ref, short_ref, cce, gce, tf, tb, mrev, mfwd, sch, xf, sacc, pick,
    part_sum, rx, xs, rz, win, rw,
    load_sem, halo_send, halo_recv, back_send, back_recv,
    x_send, x_recv, z_send, z_recv, w_send, w_recv, go, steps,
):
    n = nx * nz
    width = xe.shape[1]
    blocks = width // LANES
    groups = width // GROUP
    taps = short_ref.shape[0]
    me = lax.axis_index("ctx")
    ix, iz = me // nz, lax.rem(me, nz)

    def at_z(d):
        return ix, lax.rem(iz + d + nz, nz)

    def at_x(d):
        return lax.rem(ix + d + nx, nx), iz

    def at(d):
        other = lax.rem(me + d + n, n)
        return other // nz, lax.rem(other, nz)

    def ident(peer):
        return {"ctx": peer[0] * nz + peer[1]}

    def signal(sem, peer):
        pl.semaphore_signal(sem, inc=1, device_id=ident(peer), device_id_type=MESH)

    def lanes(b):
        return pl.ds(pl.multiple_of(b * LANES, LANES), LANES)

    loads = [
        pltpu.make_async_copy(x_hbm, xe.at[pl.ds(ROWS, ROWS)], load_sem.at[0]),
        pltpu.make_async_copy(up_hbm, upv, load_sem.at[1]),
        pltpu.make_async_copy(med_hbm, med_ref, load_sem.at[2]),
        pltpu.make_async_copy(short_hbm, short_ref, load_sem.at[3]),
    ]
    for copy in loads:
        copy.start()

    barrier = pltpu.get_barrier_semaphore()
    for peer in (at(-1), at_x(1), at_x(-1)):
        signal(barrier, peer)

    def halo(b):
        return pltpu.make_async_remote_copy(
            src_ref=xe.at[pl.ds(ROWS, ROWS), lanes(b)],
            dst_ref=xe.at[pl.ds(0, ROWS), lanes(b)],
            send_sem=halo_send.at[b],
            recv_sem=halo_recv.at[b],
            device_id=ident(at(1)),
            device_id_type=MESH,
        )

    loads[0].wait()
    pl.semaphore_wait(barrier, 3)

    @pl.when(me < n - 1)
    def _():
        for b in range(blocks):
            halo(b).start()

    @pl.when(me == n - 1)
    def _():
        signal(go, at(1))

    loads[2].wait()
    loads[3].wait()

    rows2 = lax.broadcasted_iota(jnp.int32, (ROWS, LANES), 0)
    cols2 = lax.broadcasted_iota(jnp.int32, (ROWS, LANES), 1)
    lane_group = cols2 // GROUP

    flip = (rows2 + cols2 == LANES - 1).astype(BF16)
    mrev[...] = jnp.dot(med_ref[...], flip, preferred_element_type=F32)
    mfwd[...] = med_ref[...].astype(F32)
    chan = lax.broadcasted_iota(jnp.int32, (groups, width), 1) // GROUP
    own = lax.broadcasted_iota(jnp.int32, (groups, width), 0)
    spread = (chan == own).astype(BF16)
    sch[0:taps, :] = jnp.dot(short_ref[...], spread, preferred_element_type=F32)

    above = (cols2 > rows2).astype(F32).astype(BF16)
    below = (cols2 <= rows2).astype(F32).astype(BF16)

    def forward_table(b, carry):
        for k in range(PER):
            g = b * PER + k
            row = jnp.broadcast_to(mrev[pl.ds(g, 1), :], (ROWS, LANES))
            turned = pltpu.roll(row, 1, 1, stride=1, stride_axis=0).astype(BF16)
            top = pl.ds(pl.multiple_of(g * ROWS, ROWS), ROWS)
            tf[top, 0:LANES] = turned * above
            tf[top, LANES:] = turned * below
        return carry

    def tell_sides():
        for d in (1, -1):
            signal(steps.at[0], at_x(d))

    def tell_next():
        signal(steps.at[1], at_z(-1))
        signal(steps.at[2], at_z(1))

    edge = (iz == 0) | (iz == nz - 1)

    lax.fori_loop(0, blocks, forward_table, 0)

    @pl.when(me == 0)
    def _():
        pl.semaphore_wait(go, 1)

    tall_r = lax.broadcasted_iota(jnp.int32, (width, LANES), 0) // GROUP
    tall_c = lax.broadcasted_iota(jnp.int32, (width, LANES), 1)
    pick[...] = (tall_r == tall_c).astype(BF16)

    big_r = lax.broadcasted_iota(jnp.int32, (2 * ROWS, 2 * ROWS), 0)
    big_c = lax.broadcasted_iota(jnp.int32, (2 * ROWS, 2 * ROWS), 1)
    flip_rows = (big_r + big_c == 2 * ROWS - 1).astype(BF16)

    loads[1].wait()

    def block(b, carry):
        @pl.when(me > 0)
        def _():
            halo(b).wait_recv()

        @pl.when(me == 0)
        def _():
            xe[pl.ds(0, ROWS), lanes(b)] = jnp.zeros((ROWS, LANES), BF16)

        xb = xe[:, lanes(b)]
        xf[...] = xe[pl.ds(ROWS - 16, ROWS + 16), lanes(b)].astype(F32)
        gate = jnp.zeros((ROWS, LANES), F32)
        for j in range(taps):
            gate = gate + sch[j : j + 1, lanes(b)] * xf[16 - j : 16 - j + ROWS, :]
        conv = jnp.zeros((ROWS, LANES), F32)
        for k in range(PER):
            top = pl.ds(pl.multiple_of((b * PER + k) * ROWS, ROWS), ROWS)
            term = jnp.dot(tf[top, :], xb, preferred_element_type=F32)
            conv = jnp.where(lane_group == k, term, conv)
        up = upv[:, lanes(b)].astype(F32)
        gate_cot = (up * conv).astype(BF16)
        conv_cot = (up * gate).astype(BF16)
        cce[0:ROWS, lanes(b)] = conv_cot
        gce[0:ROWS, lanes(b)] = gate_cot
        gate_f = gate_cot.astype(F32)
        for j in range(taps):
            sacc[j : j + 1, lanes(b)] = jnp.sum(
                gate_f * xf[16 - j : 16 - j + ROWS, :], axis=0, keepdims=True
            )
        x_rev = jnp.dot(flip_rows, xb, preferred_element_type=F32).astype(BF16)
        for k in range(PER):
            part = jnp.where(lane_group == k, conv_cot, jnp.zeros((), BF16))
            pair = nt(part, x_rev)
            both = jnp.where(rows2 + cols2 >= LANES - 1, pair[:, :LANES], pair[:, LANES:])
            turned = pltpu.roll(both, 1, 1, stride=1, stride_axis=0)
            part_sum[pl.ds(b * PER + k, 1), :] = jnp.sum(turned, axis=0, keepdims=True)
        @pl.when(b == 0)
        def _():
            tell_sides()
            pl.when(jnp.logical_not(edge))(tell_next)

        @pl.when(b == 2)
        def _():
            pl.semaphore_wait(steps.at[0], 2)
            pl.when(edge)(tell_next)

        return carry

    sacc[...] = jnp.zeros_like(sacc)
    lax.fori_loop(0, blocks, block, 0)

    sums = sacc[...]
    top = sums.astype(BF16)
    rest = sums - top.astype(F32)
    middle = rest.astype(BF16)
    low = (rest - middle.astype(F32)).astype(BF16)
    pieces = [jnp.dot(p, pick[...], preferred_element_type=F32) for p in (top, middle, low)]
    part_sum[groups : groups + 8, :] = pieces[0] + (pieces[1] + pieces[2])
    rx[ix] = part_sum[...].astype(BF16)

    def remote(src, dst, send, recv, peer):
        return pltpu.make_async_remote_copy(
            src_ref=src, dst_ref=dst, send_sem=send, recv_sem=recv, device_id=ident(peer), device_id_type=MESH
        )

    x_sends = [
        remote(rx.at[ix], rx.at[ix], x_send.at[d - 1], x_recv.at[d - 1], at_x(d)) for d in (2, 1, 3)
    ]
    for copy in x_sends:
        copy.start()
    back_c = remote(
        cce.at[pl.ds(0, ROWS)], cce.at[pl.ds(ROWS, ROWS)], back_send.at[0], back_recv.at[0], at(-1)
    )
    back_g = remote(
        gce.at[pl.ds(0, 16)], gce.at[pl.ds(ROWS, 16)], back_send.at[1], back_recv.at[1], at(-1)
    )

    @pl.when(me > 0)
    def _():
        back_g.start()
        back_c.start()

    strict = (cols2 < rows2).astype(F32).astype(BF16)
    upper = (cols2 >= rows2).astype(F32).astype(BF16)

    def backward_table(b, carry):
        for k in range(PER):
            g = b * PER + k
            row = jnp.broadcast_to(mfwd[pl.ds(g, 1), :], (ROWS, LANES))
            turned = pltpu.roll(row, 0, 1, stride=1, stride_axis=0).astype(BF16)
            top = pl.ds(pl.multiple_of(g * ROWS, ROWS), ROWS)
            tb[top, 0:LANES] = turned * upper
            tb[top, LANES:] = turned * strict
        return carry

    pl.semaphore_wait(steps.at[1], 1)
    lax.fori_loop(0, blocks, backward_table, 0)
    pl.semaphore_wait(steps.at[2], 1)
    signal(steps.at[3], at_z(-2))
    signal(steps.at[4], at_z(2))

    for d in range(1, nx):
        source = lax.rem(ix - d + nx, nx)
        remote(rx.at[ix], rx.at[source], x_send.at[d - 1], x_recv.at[d - 1], at_x(d)).wait_recv()
    total = part_sum[...]
    for d in range(1, nx):
        total = total + rx[lax.rem(ix + d, nx)].astype(F32)
    xs[...] = total.astype(BF16)
    z_sends = [remote(xs, rz.at[k], z_send.at[k], z_recv.at[k], at_z(d)) for k, d in enumerate(RAW)]
    z_sends[0].start()
    z_sends[1].start()
    pl.semaphore_wait(steps.at[3], 1)
    z_sends[2].start()
    pl.semaphore_wait(steps.at[4], 1)
    signal(steps.at[5], at_z(4))
    for copy in z_sends:
        copy.wait_recv()
    window = (total + rz[0].astype(F32)) + (rz[1].astype(F32) + rz[2].astype(F32))
    win[...] = window.astype(BF16)
    tot_ref[...] = window
    w_sends = [remote(win, rw.at[k], w_send.at[k], w_recv.at[k], at_z(d)) for k, d in enumerate(WIDE)]
    for copy in w_sends[:2]:
        copy.start()
    pl.semaphore_wait(steps.at[5], 1)
    w_sends[2].start()

    @pl.when(me < n - 1)
    def _():
        back_g.wait_recv()
        back_c.wait_recv()

    @pl.when(me == n - 1)
    def _():
        cce[pl.ds(ROWS, ROWS), :] = jnp.zeros((ROWS, width), BF16)
        gce[pl.ds(ROWS, 16), :] = jnp.zeros((16, width), BF16)

    def gradient(b, carry):
        cb = cce[:, lanes(b)]
        back = jnp.zeros((ROWS, LANES), F32)
        for k in range(PER):
            top = pl.ds(pl.multiple_of((b * PER + k) * ROWS, ROWS), ROWS)
            term = jnp.dot(tb[top, :], cb, preferred_element_type=F32)
            back = jnp.where(lane_group == k, term, back)
        xf[...] = gce[:, lanes(b)].astype(F32)
        short = jnp.zeros((ROWS, LANES), F32)
        for j in range(taps):
            short = short + sch[j : j + 1, lanes(b)] * xf[j : j + ROWS, :]
        igv[:, lanes(b)] = (back + short).astype(BF16)
        return carry

    lax.fori_loop(0, blocks, gradient, 0)

    for copy in w_sends:
        copy.wait_recv()
    tot_ref[...] = (tot_ref[...] + rw[0].astype(F32)) + (rw[1].astype(F32) + rw[2].astype(F32))

    @pl.when(me < n - 1)
    def _():
        for b in range(blocks):
            halo(b).wait_send()

    @pl.when(me > 0)
    def _():
        back_g.wait_send()
        back_c.wait_send()

    for copy in x_sends + z_sends + w_sends:
        copy.wait_send()


def finish(factor, ig_ref, tot_ref, ig_hbm, med_hbm, short_hbm, med_v, short_v, sems):
    groups, taps = med_v.shape[0], short_v.shape[0]
    big = pltpu.make_async_copy(ig_ref, ig_hbm, sems.at[0])
    big.start()
    med_v[...] = tot_ref[0:groups, :] * factor
    medium = pltpu.make_async_copy(med_v, med_hbm, sems.at[1])
    medium.start()
    short_v[...] = tot_ref[groups : groups + taps, 0:groups] * factor
    short = pltpu.make_async_copy(short_v, short_hbm, sems.at[2])
    short.start()
    big.wait()
    medium.wait()
    short.wait()


def local(nx, nz, inputs, upstream, medium_filter, short_filter):
    rows, width = inputs.shape
    groups, taps = medium_filter.shape
    short_taps = short_filter.shape[1]
    if rows != ROWS or taps != LANES or width % LANES or groups != 32:
        raise ValueError("unsupported sizes")
    height = groups + 8
    blocks = width // LANES
    vmem = pltpu.VMEM
    dma = pltpu.SemaphoreType.DMA
    hbm = pl.BlockSpec(memory_space=pl.ANY)
    local_mem = pl.BlockSpec(memory_space=pltpu.VMEM)
    gradient, total = pl.pallas_call(
        functools.partial(kernel, nx, nz),
        out_shape=(vmem((rows, width), BF16), vmem((height, LANES), F32)),
        in_specs=[hbm] * 4,
        out_specs=(local_mem, local_mem),
        scratch_shapes=[
            vmem((2 * ROWS, width), BF16),
            vmem((ROWS, width), BF16),
            vmem((groups, LANES), BF16),
            vmem((short_taps, groups), BF16),
            vmem((2 * ROWS, width), BF16),
            vmem((ROWS + 16, width), BF16),
            vmem((groups * ROWS, 2 * LANES), BF16),
            vmem((groups * ROWS, 2 * LANES), BF16),
            vmem((groups, LANES), F32),
            vmem((groups, LANES), F32),
            vmem((8, width), F32),
            vmem((ROWS + 16, LANES), F32),
            vmem((8, width), F32),
            vmem((width, LANES), BF16),
            vmem((height, LANES), F32),
            vmem((nx, height, LANES), BF16),
            vmem((height, LANES), BF16),
            vmem((len(RAW), height, LANES), BF16),
            vmem((height, LANES), BF16),
            vmem((len(WIDE), height, LANES), BF16),
            dma((4,)),
            dma((blocks,)),
            dma((blocks,)),
            dma((2,)),
            dma((2,)),
            dma((nx - 1,)),
            dma((nx - 1,)),
            dma((len(RAW),)),
            dma((len(RAW),)),
            dma((len(WIDE),)),
            dma((len(WIDE),)),
            pltpu.SemaphoreType.REGULAR,
            pltpu.SemaphoreType.REGULAR((6,)),
        ],
        compiler_params=pltpu.CompilerParams(collective_id=0, has_side_effects=True),
    )(inputs, upstream, medium_filter, short_filter.T)
    factor = float(GROUP * rows * lax.axis_size("ctx")) ** (-0.5)
    gradient, medium, short = pl.pallas_call(
        functools.partial(finish, factor),
        out_shape=(
            jax.ShapeDtypeStruct((rows, width), BF16),
            jax.ShapeDtypeStruct((groups, LANES), F32),
            jax.ShapeDtypeStruct((short_taps, groups), F32),
        ),
        in_specs=[local_mem, local_mem],
        out_specs=(hbm, hbm, hbm),
        scratch_shapes=[vmem((groups, LANES), F32), vmem((short_taps, groups), F32), dma((3,))],
    )(pltpu.with_memory_space_constraint(gradient, pltpu.VMEM), pltpu.with_memory_space_constraint(total, pltpu.VMEM))
    return gradient, medium, short.T


def solution(mesh):
    n = mesh.shape["ctx"]
    nz = 16
    return jax.shard_map(
        functools.partial(local, n // nz, nz),
        mesh=mesh,
        in_specs=(P("ctx", "fsdp"), P("ctx", "fsdp"), P("fsdp", None), P("fsdp", None)),
        out_specs=(P("ctx", "fsdp"), P("fsdp", None), P("fsdp", None)),
        check_vma=False,
    )
```
